32 devices in a mesh: replica: 8 (over z, y), shard: 4 (over x, core).
Axes of the slice: x: 2, y: 2, z: 4, core: 2. Of those that a mesh axis runs over, the one named last changes fastest.
Arguments:
- hidden_in: bfloat16 [4096, 1024], P(('replica', 'shard')), may hold values from -6 to 6
- out_grad: bfloat16 [4096, 1024], P(('replica', 'shard')), may hold values from -6 to 6
- lengths: int32 [32, 4], P(('replica', 'shard')), may hold values from 1 to 64, 128 in all within a row
- norm1_gain: bfloat16 [1024], P('shard'), may hold values from 0.099609375 to 1.8984375
- norm1_bias: bfloat16 [1024], P('shard'), may hold values from -3 to 3
- qkv_weight: bfloat16 [1024, 3072], P('shard'), may hold values from -0.1875 to 0.1875
- query_bias: bfloat16 [1024], P('shard'), may hold values from -3 to 3
- value_bias: bfloat16 [1024], P('shard'), may hold values from -3 to 3
- out_weight: bfloat16 [1024, 1024], P('shard'), may hold values from -0.75 to 0.75
- out_bias: bfloat16 [1024], P('shard'), may hold values from -3 to 3
- norm2_gain: bfloat16 [1024], P('shard'), may hold values from 0.099609375 to 1.8984375
- norm2_bias: bfloat16 [1024], P('shard'), may hold values from -3 to 3
- up_weight: bfloat16 [1024, 4096], P('shard'), may hold values from -0.1875 to 0.1875
- up_bias: bfloat16 [4096], P('shard'), may hold values from -3 to 3
- down_weight: bfloat16 [4096, 1024], P('shard'), may hold values from -0.125 to 0.125
- down_bias: bfloat16 [1024], P('shard'), may hold values from -3 to 3
Outputs:
- hidden_out: bfloat16 [4096, 1024], P(('replica', 'shard'))
- in_grad: bfloat16 [4096, 1024], P(('replica', 'shard'))
- norm1_gain_grad: float32 [1024], P('shard')
- norm1_bias_grad: float32 [1024], P('shard')
- qkv_weight_grad: float32 [1024, 3072], P('shard')
- query_bias_grad: float32 [1024], P('shard')
- value_bias_grad: float32 [1024], P('shard')
- out_weight_grad: float32 [1024, 1024], P('shard')
- out_bias_grad: float32 [1024], P('shard')
- norm2_gain_grad: float32 [1024], P('shard')
- norm2_bias_grad: float32 [1024], P('shard')
- up_weight_grad: float32 [1024, 4096], P('shard')
- up_bias_grad: float32 [4096], P('shard')
- down_weight_grad: float32 [4096, 1024], P('shard')
- down_bias_grad: float32 [1024], P('shard')
The draws below stay inside these ranges and needn't reach their ends.
Inputs may be any that keep to these rules, and one draw needn't show every extreme that they name: The 4 lengths of each device add up to 128, and the largest of all is 64.
All inputs are finite; a program needn't handle non-finite values.
Results may differ from the reference program's by a relative error of at most 0.018.
Values may be sent and summed in bfloat16 or wider, within the bound.
A program may use at most 192 MiB of HBM per device.

```python
import math
import jax
import jax.numpy as jnp
import numpy as np
from jax import lax

D = 1024
HEADS = 16
HEAD_DIM = 64
FF = 4096
TOK_DEV = 128
SEQS = 4
MOST = 64
TOKENS = 4096
N_REPLICA = 8
N_SHARD = 4


def block_levels(stream_key, shape, cuts, smallest, high):
    loudness = 1.0
    for position, parts in cuts:
        steps = jax.random.uniform(jax.random.fold_in(jax.random.fold_in(stream_key, 6), position), (parts,), jnp.float32, smallest / len(cuts), high / len(cuts))
        loudness = loudness * jnp.repeat(jnp.exp(steps), shape[position] // parts).reshape((-1,) + (1,) * (len(shape) - 1 - position))
    return loudness


def split_up(count, total, reach, slope):
    loads = [(1 << 20) // math.isqrt(grade ** slope) + 1 for grade in range(2, count + 1)]
    rest, counts = total - reach - (count - 1), [1] * (count - 1)
    while rest > 0:
        movable = [i for i in range(count - 1) if counts[i] < reach]
        mass, budget = sum([loads[i] for i in movable]), rest
        for i in movable:
            extra = min(reach - counts[i], max(1, budget * loads[i] // mass), rest)
            counts[i] = counts[i] + extra
            rest = rest - extra
    return np.array([reach] + counts)


def uneven_parts(key, amount, total, limit, lean):
    if amount == 2:
        one = jax.random.randint(key, (), max(1, total - limit), min(limit, total - 1) + 1)
        return jnp.stack([one, total - one])
    sizes = jnp.asarray(split_up(amount, total, limit, lean), jnp.int32)
    couples = (amount - 1) // 2
    giver, sink = sizes[1:1 + 2 * couples:2], sizes[2:2 + 2 * couples:2]
    room = jnp.minimum(giver - 1, limit - sink)
    shifted = jax.random.randint(jax.random.fold_in(key, 1), (couples,), 0, 1 << 20) % (room + 1)
    sizes = sizes.at[1:1 + 2 * couples:2].set(giver - shifted).at[2:2 + 2 * couples:2].set(sink + shifted)
    return sizes[jax.random.permutation(jax.random.fold_in(key, 2), amount)]


def normal_values(rng, dims, scale, reach, split=(), held_as=jnp.bfloat16):
    drawn = scale * jax.random.normal(rng, dims, jnp.float32)
    if split:
        drawn = drawn * block_levels(rng, dims, split, -0.22, 0.18)
    return jnp.clip(drawn, -reach, reach).astype(held_as)


def setup_inputs(seed: int = 0) -> dict:
    streams_of = jax.random.split(jax.random.key(seed), 17)
    hidden_in = normal_values(streams_of[0], (TOKENS, D), 1.0, 6.0, ((0, 32),))
    out_grad = normal_values(streams_of[1], (TOKENS, D), 1.0, 6.0, ((0, 32),))
    lengths = jax.vmap(lambda own: uneven_parts(own, SEQS, TOK_DEV, MOST, 2))(jax.random.split(streams_of[2], (N_REPLICA * N_SHARD))).reshape((N_REPLICA * N_SHARD, SEQS)).astype(jnp.int32)
    norm1_gain = jnp.clip(1.0 + 0.18 * jax.random.normal(streams_of[3], (D,), jnp.float32), 0.099609375, 1.8984375).astype(jnp.bfloat16)
    norm1_bias = normal_values(streams_of[4], (D,), 0.5, 3.0, ((0, 4),))
    qkv_weight = normal_values(streams_of[5], (D, 3 * D), D ** -0.5, 0.1875, ((0, 4),))
    query_bias = normal_values(streams_of[6], (D,), 0.5, 3.0, ((0, 4),))
    value_bias = normal_values(streams_of[7], (D,), 0.5, 3.0, ((0, 4),))
    out_weight = normal_values(streams_of[8], (D, D), (D // 16) ** -0.5, 0.75, ((0, 4),))
    out_bias = normal_values(streams_of[9], (D,), 0.5, 3.0, ((0, 4),))
    norm2_gain = jnp.clip(1.0 + 0.18 * jax.random.normal(streams_of[10], (D,), jnp.float32), 0.099609375, 1.8984375).astype(jnp.bfloat16)
    norm2_bias = normal_values(streams_of[11], (D,), 0.5, 3.0, ((0, 4),))
    up_weight = normal_values(streams_of[12], (D, FF), D ** -0.5, 0.1875, ((0, 4),))
    up_bias = normal_values(streams_of[13], (FF,), 0.5, 3.0, ((0, 4),))
    down_weight = normal_values(streams_of[14], (FF, D), (FF // 2) ** -0.5, 0.125, ((0, 4),))
    down_bias = normal_values(streams_of[15], (D,), 0.5, 3.0, ((0, 4),))
    return {"hidden_in": hidden_in, "out_grad": out_grad, "lengths": lengths, "norm1_gain": norm1_gain, "norm1_bias": norm1_bias, "qkv_weight": qkv_weight, "query_bias": query_bias, "value_bias": value_bias, "out_weight": out_weight, "out_bias": out_bias, "norm2_gain": norm2_gain, "norm2_bias": norm2_bias, "up_weight": up_weight, "up_bias": up_bias, "down_weight": down_weight, "down_bias": down_bias}


EPSILON = 1e-05
TANH_SCALE = math.sqrt(2.0 / math.pi)
CUBIC = 0.044715

def round_trip(source):
    return lax.optimization_barrier(source.astype(jnp.bfloat16)).astype(jnp.float32)

def product(left, right):
    return jnp.dot(left, right, preferred_element_type=jnp.float32)

def left_product(left, right):
    return jnp.dot(left.T, right, preferred_element_type=jnp.float32)

def right_product(left, right):
    return jnp.dot(left, right.T, preferred_element_type=jnp.float32)

def gelu_parts(pre_act):
    inner_arg = TANH_SCALE * (pre_act + CUBIC * pre_act * pre_act * pre_act)
    tangent = jnp.tanh(inner_arg)
    gelu_value = 0.5 * pre_act * (1.0 + tangent)
    gelu_slope = 0.5 * (1.0 + tangent) + 0.5 * pre_act * (1.0 - tangent * tangent) * TANH_SCALE * (1.0 + 3.0 * CUBIC * pre_act * pre_act)
    return (gelu_value, gelu_slope)

def layer_norm(inputs, gain_row, bias_row):
    average = lax.optimization_barrier(jnp.mean(inputs, axis=-1, keepdims=True))
    centred = inputs - average
    inv_std = lax.rsqrt(lax.optimization_barrier(jnp.mean(centred * centred, axis=-1, keepdims=True)) + EPSILON)
    normed = centred * inv_std
    return (normed * gain_row.astype(jnp.float32) + bias_row.astype(jnp.float32), normed, inv_std)

def norm_back(upstream, normed, inv_std, gain_row):
    scaled = upstream * gain_row.astype(jnp.float32)
    first_term = lax.optimization_barrier(jnp.mean(scaled, axis=-1, keepdims=True))
    second_term = lax.optimization_barrier(jnp.mean(scaled * normed, axis=-1, keepdims=True))
    input_grad = inv_std * (scaled - first_term - normed * second_term)
    return (input_grad, lax.optimization_barrier(jnp.sum(upstream * normed, axis=0)), lax.optimization_barrier(jnp.sum(upstream, axis=0)))

def seq_mask(lengths, row_count):
    seq_ends = jnp.cumsum(lengths, axis=-1).astype(jnp.int32)
    places = jnp.arange(row_count, dtype=jnp.int32)
    segment = lax.optimization_barrier(jnp.sum((places[None, :, None] >= seq_ends[:, None, :]).astype(jnp.int32), axis=-1))
    causal = places[None, :] <= places[:, None]
    return (segment[:, :, None] == segment[:, None, :]) & causal[None]

def split_heads(flat_rows, groups):
    return flat_rows.reshape(groups, -1, HEADS, HEAD_DIM).astype(jnp.float32)

def attend_forward(queries, key_rows, values, allowed):
    groups = allowed.shape[0]
    scale_factor = 1.0 / math.sqrt(HEAD_DIM)
    head_q = split_heads(queries, groups)
    head_k = split_heads(key_rows, groups)
    head_v = split_heads(values, groups)
    scores = jnp.einsum('gqhd,gkhd->ghqk', head_q, head_k) * scale_factor
    visible = allowed[:, None]
    row_total = lax.optimization_barrier(jnp.sum(jnp.where(visible, jnp.exp(scores), 0.0), axis=-1, keepdims=True))
    log_total = jnp.log(row_total)
    probs_round = round_trip(jnp.where(visible, jnp.exp(scores - log_total), 0.0))
    context = jnp.einsum('ghqk,gkhd->gqhd', probs_round, head_v)
    return (context.reshape(-1, HEADS * HEAD_DIM).astype(jnp.bfloat16), log_total)

def attend_backward(queries, key_rows, values, allowed, log_total, context_grad):
    groups = allowed.shape[0]
    scale_factor = 1.0 / math.sqrt(HEAD_DIM)
    head_q = split_heads(queries, groups)
    head_k = split_heads(key_rows, groups)
    head_v = split_heads(values, groups)
    head_g = split_heads(context_grad, groups)
    scores = jnp.einsum('gqhd,gkhd->ghqk', head_q, head_k) * scale_factor
    visible = allowed[:, None]
    exact_probs = jnp.where(visible, jnp.exp(scores - log_total), 0.0)
    probs_round = round_trip(exact_probs)
    prob_grad = jnp.einsum('gqhd,gkhd->ghqk', head_g, head_v)
    value_grad = jnp.einsum('ghqk,gqhd->gkhd', probs_round, head_g)
    row_delta = lax.optimization_barrier(jnp.sum(exact_probs * prob_grad, axis=-1, keepdims=True))
    score_grad = round_trip(exact_probs * (prob_grad - row_delta) * scale_factor)
    query_grad = jnp.einsum('ghqk,gkhd->gqhd', score_grad, head_k)
    key_grad = jnp.einsum('ghqk,gqhd->gkhd', score_grad, head_q)
    model_width = HEADS * HEAD_DIM
    return (query_grad.reshape(-1, model_width), key_grad.reshape(-1, model_width), value_grad.reshape(-1, model_width))

def whole_block(inputs, out_grad, allowed, weights_all):
    norm1_gain, norm1_bias, qkv_weight, query_bias, value_bias, out_weight, out_bias, norm2_gain, norm2_bias, up_weight, up_bias, down_weight, down_bias = weights_all
    model_width = inputs.shape[1]
    inputs_wide = inputs.astype(jnp.float32)
    first_out, normed_one, inv_one = layer_norm(inputs_wide, norm1_gain, norm1_bias)
    first_in = first_out.astype(jnp.bfloat16)
    projected = product(first_in, qkv_weight)
    queries = (projected[:, :model_width] + query_bias.astype(jnp.float32)).astype(jnp.bfloat16)
    key_rows = projected[:, model_width:2 * model_width].astype(jnp.bfloat16)
    values = (projected[:, 2 * model_width:] + value_bias.astype(jnp.float32)).astype(jnp.bfloat16)
    context, log_total = attend_forward(queries, key_rows, values, allowed)
    residual = inputs_wide + product(context, out_weight) + out_bias.astype(jnp.float32)
    second_out, normed_two, inv_two = layer_norm(residual, norm2_gain, norm2_bias)
    second_in = second_out.astype(jnp.bfloat16)
    pre_act = product(second_in, up_weight) + up_bias.astype(jnp.float32)
    activ_value, gelu_slope = gelu_parts(pre_act)
    activated = activ_value.astype(jnp.bfloat16)
    hidden_out = (residual + product(activated, down_weight) + down_bias.astype(jnp.float32)).astype(jnp.bfloat16)
    upstream = out_grad.astype(jnp.float32)
    down_wgrad = round_trip(left_product(activated, out_grad))
    down_bgrad = lax.optimization_barrier(jnp.sum(upstream, axis=0))
    pre_grad = right_product(out_grad, down_weight) * gelu_slope
    pre_round = pre_grad.astype(jnp.bfloat16)
    up_bgrad = lax.optimization_barrier(jnp.sum(pre_grad, axis=0))
    up_wgrad = round_trip(left_product(second_in, pre_round))
    second_grad = right_product(pre_round, up_weight)
    norm_two_in, gain2_grad, bias2_grad = norm_back(second_grad, normed_two, inv_two, norm2_gain)
    resid_grad = upstream + norm_two_in
    resid_round = resid_grad.astype(jnp.bfloat16)
    out_bgrad = lax.optimization_barrier(jnp.sum(resid_grad, axis=0))
    out_wgrad = round_trip(left_product(context, resid_round))
    context_grad = right_product(resid_round, out_weight).astype(jnp.bfloat16)
    query_grad, key_grad, value_grad = attend_backward(queries, key_rows, values, allowed, log_total, context_grad)
    query_bgrad = lax.optimization_barrier(jnp.sum(query_grad, axis=0))
    value_bgrad = lax.optimization_barrier(jnp.sum(value_grad, axis=0))
    qkv_grad = jnp.concatenate([query_grad, key_grad, value_grad], axis=1).astype(jnp.bfloat16)
    qkv_wgrad = round_trip(left_product(first_in, qkv_grad))
    first_grad = right_product(qkv_grad, qkv_weight)
    norm_one_in, gain1_grad, bias1_grad = norm_back(first_grad, normed_one, inv_one, norm1_gain)
    in_grad = (resid_grad + norm_one_in).astype(jnp.bfloat16)
    grads_all = (gain1_grad, bias1_grad, qkv_wgrad, query_bgrad, value_bgrad, out_wgrad, out_bgrad, gain2_grad, bias2_grad, up_wgrad, up_bgrad, down_wgrad, down_bgrad)
    return (hidden_out, in_grad, grads_all)

def reference(hidden_in, out_grad, lengths, norm1_gain, norm1_bias, qkv_weight, query_bias, value_bias, out_weight, out_bias, norm2_gain, norm2_bias, up_weight, up_bias, down_weight, down_bias):
    weights_all = (norm1_gain, norm1_bias, qkv_weight, query_bias, value_bias, out_weight, out_bias, norm2_gain, norm2_bias, up_weight, up_bias, down_weight, down_bias)
    device_count = lengths.shape[0]
    tok_count = hidden_in.shape[0] // device_count
    model_width = hidden_in.shape[1]
    inputs_all = hidden_in.reshape(device_count, tok_count, model_width)
    cotan_all = out_grad.reshape(device_count, tok_count, model_width)
    lengths_all = lengths.reshape(device_count, 1, lengths.shape[1])

    def advance(totals, element):
        inputs, cotan, lengths_now = element
        allowed = seq_mask(lengths_now, tok_count)
        hidden_out, in_grad, grads_all = whole_block(inputs, cotan, allowed, weights_all)
        return (tuple((total + grad for total, grad in zip(totals, grads_all))), (hidden_out, in_grad))
    initial = tuple((jnp.zeros(weight.shape, jnp.float32) for weight in weights_all))
    totals, (outs_all, grads_in) = lax.scan(advance, initial, (inputs_all, cotan_all, lengths_all))
    return (outs_all.reshape(hidden_in.shape), grads_in.reshape(hidden_in.shape), totals[0], totals[1], totals[2], totals[3], totals[4], totals[5], totals[6], totals[7], totals[8], totals[9], totals[10], totals[11], totals[12])
```

```python
import functools
import math

import jax
import jax.numpy as jnp
from jax import lax
from jax.experimental import pallas as pl
from jax.experimental.pallas import tpu as pltpu
from jax.sharding import PartitionSpec as P

HEADS = 16
HEAD_DIM = 64


EPSILON = 1e-05
TANH_SCALE = math.sqrt(2.0 / math.pi)
CUBIC = 0.044715


def product(left, right):
    return jnp.dot(left, right, preferred_element_type=jnp.float32)


def left_product(left, right):
    return lax.dot_general(
        left, right, (((0,), (0,)), ((), ())), preferred_element_type=jnp.float32
    )


def right_product(left, right):
    return lax.dot_general(
        left, right, (((1,), (1,)), ((), ())), preferred_element_type=jnp.float32
    )


def column_term(left, right):
    return left_product(left, right)


def gelu_parts(pre_act):
    inner_arg = TANH_SCALE * (pre_act + CUBIC * pre_act * pre_act * pre_act)
    tangent = jnp.tanh(inner_arg)
    gelu_value = 0.5 * pre_act * (1.0 + tangent)
    gelu_slope = 0.5 * (1.0 + tangent) + 0.5 * pre_act * (1.0 - tangent * tangent) * TANH_SCALE * (
        1.0 + 3.0 * CUBIC * pre_act * pre_act
    )
    return (gelu_value, gelu_slope)


def layer_norm(inputs, gain_row, bias_row):
    average = jnp.mean(inputs, axis=-1, keepdims=True)
    centred = inputs - average
    inv_std = lax.rsqrt(jnp.mean(centred * centred, axis=-1, keepdims=True) + EPSILON)
    normed = centred * inv_std
    return (normed * gain_row.astype(jnp.float32) + bias_row.astype(jnp.float32), normed, inv_std)


def norm_back(upstream, normed, inv_std, gain_row):
    scaled = upstream * gain_row.astype(jnp.float32)
    first_term = jnp.mean(scaled, axis=-1, keepdims=True)
    second_term = jnp.mean(scaled * normed, axis=-1, keepdims=True)
    input_grad = inv_std * (scaled - first_term - normed * second_term)
    return (input_grad, jnp.sum(upstream * normed, axis=0), jnp.sum(upstream, axis=0))


def seq_mask(lengths, row_count):
    seq_ends = jnp.cumsum(lengths, axis=-1)
    places = jnp.arange(row_count, dtype=jnp.int32)
    segment = jnp.sum((places[None, :, None] >= seq_ends[:, None, :]).astype(jnp.int32), axis=-1)
    causal = places[None, :] <= places[:, None]
    return (segment[:, :, None] == segment[:, None, :]) & causal[None]


def split_heads(flat_rows, groups):
    return flat_rows.reshape(groups, -1, flat_rows.shape[1] // HEAD_DIM, HEAD_DIM)


def attend_forward(queries, key_rows, values, allowed):
    groups = allowed.shape[0]
    scale_factor = 1.0 / math.sqrt(HEAD_DIM)
    head_q = split_heads(queries, groups)
    head_k = split_heads(key_rows, groups)
    head_v = split_heads(values, groups)
    scores = (
        jnp.einsum("gqhd,gkhd->ghqk", head_q, head_k, preferred_element_type=jnp.float32)
        * scale_factor
    )
    visible = allowed[:, None]
    row_total = jnp.sum(jnp.where(visible, jnp.exp(scores), 0.0), axis=-1, keepdims=True)
    log_total = jnp.log(row_total)
    probs_round = jnp.where(visible, jnp.exp(scores - log_total), 0.0).astype(jnp.bfloat16)
    context = jnp.einsum("ghqk,gkhd->gqhd", probs_round, head_v, preferred_element_type=jnp.float32)
    return (context.reshape(-1, queries.shape[1]).astype(jnp.bfloat16), log_total)


def attend_backward(queries, key_rows, values, allowed, log_total, context_grad):
    groups = allowed.shape[0]
    scale_factor = 1.0 / math.sqrt(HEAD_DIM)
    head_q = split_heads(queries, groups)
    head_k = split_heads(key_rows, groups)
    head_v = split_heads(values, groups)
    head_g = split_heads(context_grad, groups)
    scores = (
        jnp.einsum("gqhd,gkhd->ghqk", head_q, head_k, preferred_element_type=jnp.float32)
        * scale_factor
    )
    visible = allowed[:, None]
    exact_probs = jnp.where(visible, jnp.exp(scores - log_total), 0.0)
    probs_round = exact_probs.astype(jnp.bfloat16)
    prob_grad = jnp.einsum("gqhd,gkhd->ghqk", head_g, head_v, preferred_element_type=jnp.float32)
    value_grad = jnp.einsum(
        "ghqk,gqhd->gkhd", probs_round, head_g, preferred_element_type=jnp.float32
    )
    row_delta = jnp.sum(exact_probs * prob_grad, axis=-1, keepdims=True)
    score_grad = (exact_probs * (prob_grad - row_delta) * scale_factor).astype(jnp.bfloat16)
    query_grad = jnp.einsum(
        "ghqk,gkhd->gqhd", score_grad, head_k, preferred_element_type=jnp.float32
    )
    key_grad = jnp.einsum("ghqk,gqhd->gkhd", score_grad, head_q, preferred_element_type=jnp.float32)
    model_width = queries.shape[1]
    return (
        query_grad.reshape(-1, model_width),
        key_grad.reshape(-1, model_width),
        value_grad.reshape(-1, model_width),
    )


MESH = pl.DeviceIdType.MESH
VMEM_LIMIT = 60 * 1024 * 1024


def push(source, target, send_sem, recv_sem, device):
    return pltpu.make_async_remote_copy(
        src_ref=source,
        dst_ref=target,
        send_sem=send_sem,
        recv_sem=recv_sem,
        device_id=device,
        device_id_type=MESH,
    )


def greet(devices):
    barrier = pltpu.get_barrier_semaphore()
    for device in devices:
        pl.semaphore_signal(barrier, inc=1, device_id=device, device_id_type=MESH)
    pl.semaphore_wait(barrier, len(devices))


def group_peers(replica, me, size):
    return [(replica, lax.rem(me + k, size)) for k in range(1, size)]


class Spread:
    def __init__(self, blocks, replica, me, size, send, recv):
        core = lax.rem(me, 2)
        outer = me // 2
        half = size // 2
        self.partner = (replica, me + 1 - 2 * core)
        self.blocks, self.me, self.send, self.recv = blocks, me, send, recv
        self.size = size
        others = [lax.rem(outer + k, half) for k in range(1, half)]
        self.mates = [2 * j + core for j in others]
        self.far = [2 * j + 1 - core for j in others]
        self.replica = replica
        self.count = half

    def copy(self, k, block, device):
        return push(
            self.blocks.at[block], self.blocks.at[block], self.send.at[k], self.recv.at[block], device
        )

    def start(self):
        for k, mate in enumerate(self.mates):
            self.copy(k, self.me, (self.replica, mate)).start()
        self.copy(self.count, self.me, self.partner).start()

    def forward(self):
        for k, mate in enumerate(self.mates):
            self.copy(k, mate, self.partner).wait_recv()
            self.copy(self.count + 1 + k, mate, self.partner).start()

    def finish(self):
        for block in [self.partner[1]] + self.far:
            self.copy(0, block, self.partner).wait_recv()
        for k in range(len(self.mates)):
            self.copy(k, self.me, self.partner).wait_send()
            self.copy(self.count + 1 + k, self.me, self.partner).wait_send()
        self.copy(self.count, self.me, self.partner).wait_send()


def opening_kernel(size, hid_ref, grad_ref, par_ref, qkv_ref, up_ref,
                   hid_out, grad_out, par_out, qkv_out, up_out,
                   g_send, g_recv, w_send, w_recv, f_send, local_sem):
    replica = lax.axis_index("replica")
    me = lax.axis_index("shard")
    twin = replica + 1 - 2 * lax.rem(replica, 2)
    part = lax.rem(replica, 2)
    core = lax.rem(me, 2)
    outer = me // 2
    half = size // 2
    partner = me + 1 - 2 * core
    greet(group_peers(replica, me, size) + [(twin, me)])
    own = []
    for i, (src, dst) in enumerate(
        ((hid_ref, hid_out), (grad_ref, grad_out), (par_ref, par_out), (qkv_ref, qkv_out), (up_ref, up_out))
    ):
        if i < 3:
            own.append(pltpu.make_async_copy(src.at[0], dst.at[me], local_sem.at[i]))
        else:
            own.append(pltpu.make_async_copy(src.at[me], dst.at[me], local_sem.at[i]))
        own[-1].start()
    spreads = [
        Spread(out, replica, me, size, g_send.at[i], g_recv.at[i])
        for i, out in enumerate((hid_out, grad_out, par_out))
    ]
    own[0].wait()
    own[2].wait()
    spreads[2].start()
    spreads[0].start()
    remote = []
    for k in range(1, half):
        j = lax.rem(outer + k, half)
        remote += [2 * j + core, 2 * j + 1 - core]
    weights = ((qkv_ref, qkv_out), (up_ref, up_out))
    first = []
    for w, (src, dst) in enumerate(weights):
        for t, target in enumerate(remote):
            copy = push(
                src.at[target, part], dst.at[me, part],
                w_send.at[w, t], w_recv.at[w, me, part], (replica, target),
            )
            copy.start()
            first.append(copy)
        for h in range(2):
            copy = push(
                src.at[partner, h], dst.at[me, h],
                w_send.at[w, len(remote) + h], w_recv.at[w, me, h], (replica, partner),
            )
            copy.start()
            first.append(copy)
    own[1].wait()
    spreads[1].start()
    spreads[2].forward()
    spreads[0].forward()
    second = []
    for w, (src, dst) in enumerate(weights):
        for t, source in enumerate(remote):
            arrived = push(
                src.at[source, part], dst.at[source, part],
                w_send.at[w, t], w_recv.at[w, source, part], (replica, source),
            )
            arrived.wait_recv()
            copy = push(
                dst.at[source, part], dst.at[source, part],
                f_send.at[w, t], w_recv.at[w, source, part], (twin, me),
            )
            copy.start()
            second.append(copy)
    spreads[1].forward()
    for w, (src, dst) in enumerate(weights):
        for source in remote:
            push(
                dst.at[source, 1 - part], dst.at[source, 1 - part],
                f_send.at[w, 0], w_recv.at[w, source, 1 - part], (twin, me),
            ).wait_recv()
        for h in range(2):
            push(
                src.at[partner, h], dst.at[partner, h],
                w_send.at[w, 0], w_recv.at[w, partner, h], (replica, partner),
            ).wait_recv()
    for copy in first + second:
        copy.wait_send()
    own[3].wait()
    own[4].wait()
    for spread in spreads:
        spread.finish()


def vmem_specs(count):
    return [pl.BlockSpec(memory_space=pltpu.VMEM)] * count


def opening(size, hidden, upstream, params, qkv_parts, up_parts):
    dma = pltpu.SemaphoreType.DMA
    shape = lambda array: jax.ShapeDtypeStruct((size,) + array.shape[1:], array.dtype)
    arrays = (hidden[None], upstream[None], params[None], qkv_parts, up_parts)
    return pl.pallas_call(
        functools.partial(opening_kernel, size),
        out_shape=tuple(shape(a) for a in arrays),
        in_specs=vmem_specs(5),
        out_specs=tuple(vmem_specs(5)),
        scratch_shapes=[
            dma((3, size)), dma((3, size)), dma((2, size)), dma((2, size, 2)), dma((2, size)), dma((5,)),
        ],
        compiler_params=pltpu.CompilerParams(
            collective_id=0, has_side_effects=True, vmem_limit_bytes=VMEM_LIMIT
        ),
    )(*arrays)


def group_sum_kernel(size, gathers, *refs):
    n = len(gathers)
    half = size // 2
    ins, outs = refs[:n], refs[n : 2 * n]
    scratch = refs[2 * n :]
    replica = lax.axis_index("replica")
    me = lax.axis_index("shard")
    core = lax.rem(me, 2)
    outer = me // 2
    partner = (replica, me + 1 - 2 * core)
    greet(group_peers(replica, me, size))
    order = [lax.rem(outer + k, half) for k in range(1, half)] + [outer]
    work = []
    for i in range(n):
        near, summed, far, p_send, p_recv, x_send, x_recv, g_send, g_recv = scratch[9 * i : 9 * i + 9]
        for k, j in enumerate(order):
            push(
                ins[i].at[2 * j + 1 - core], near.at[j], p_send.at[k], p_recv.at[j], partner
            ).start()
    for i in range(n):
        near, summed, far, p_send, p_recv, x_send, x_recv, g_send, g_recv = scratch[9 * i : 9 * i + 9]
        for k, j in enumerate(order):
            push(ins[i].at[2 * j + 1 - core], near.at[j], p_send.at[k], p_recv.at[j], partner).wait_recv()
            if k < half - 1:
                block = ins[i][2 * j + core].astype(jnp.float32) + near[j].astype(jnp.float32)
                summed[k] = block.astype(jnp.bfloat16)
                push(
                    summed.at[k], far.at[outer], x_send.at[k], x_recv.at[outer], (replica, 2 * j + core)
                ).start()
    spreads = []
    for i in range(n):
        near, summed, far, p_send, p_recv, x_send, x_recv, g_send, g_recv = scratch[9 * i : 9 * i + 9]
        total = ins[i][me].astype(jnp.float32) + near[outer].astype(jnp.float32)
        for k, j in enumerate(order[:-1]):
            push(
                summed.at[k], far.at[j], x_send.at[k], x_recv.at[j], (replica, 2 * j + core)
            ).wait_recv()
            total = total + far[j].astype(jnp.float32)
        if gathers[i]:
            outs[i][me] = total.astype(outs[i].dtype)
            spread = Spread(outs[i], replica, me, size, g_send, g_recv)
            spread.start()
            spreads.append(spread)
        else:
            outs[i][...] = total.astype(outs[i].dtype)
    for spread in spreads:
        spread.forward()
    for spread in spreads:
        spread.finish()
    for i in range(n):
        near, summed, far, p_send, p_recv, x_send, x_recv, g_send, g_recv = scratch[9 * i : 9 * i + 9]
        for k, j in enumerate(order):
            push(ins[i].at[2 * j + 1 - core], near.at[j], p_send.at[k], p_recv.at[j], partner).wait_send()
            if k < half - 1:
                push(
                    summed.at[k], far.at[outer], x_send.at[k], x_recv.at[outer], (replica, 2 * j + core)
                ).wait_send()


def group_sum(size, partials, gathers, collective):
    dma = pltpu.SemaphoreType.DMA
    half = size // 2
    shapes, scratch, blocks = [], [], []
    for partial, gather in zip(partials, gathers):
        block = partial.reshape(size, -1, partial.shape[-1])
        blocks.append(block)
        if gather:
            shapes.append(jax.ShapeDtypeStruct(block.shape, jnp.bfloat16))
        else:
            shapes.append(jax.ShapeDtypeStruct(block.shape[1:], jnp.float32))
        for _ in range(3):
            scratch.append(pltpu.VMEM((half,) + block.shape[1:], jnp.bfloat16))
        scratch += [dma((half,)), dma((half,)), dma((half,)), dma((half,)), dma((size,)), dma((size,))]
    return pl.pallas_call(
        functools.partial(group_sum_kernel, size, gathers),
        out_shape=tuple(shapes),
        in_specs=vmem_specs(len(blocks)),
        out_specs=tuple(vmem_specs(len(blocks))),
        scratch_shapes=scratch,
        compiler_params=pltpu.CompilerParams(
            collective_id=collective, has_side_effects=True, vmem_limit_bytes=VMEM_LIMIT
        ),
    )(*blocks)


KEEP, SWAP, ADD = 0, 1, 2


def closing_kernel(size, ring, modes, *refs):
    n = len(modes)
    ins, outs, lands = refs[:n], refs[n : 2 * n], refs[2 * n : 3 * n]
    swaps = refs[3 * n : 4 * n]
    r_send, r_recv, a_send, a_recv, s_send, s_recv = refs[4 * n :]
    replica = lax.axis_index("replica")
    me = lax.axis_index("shard")
    side = lax.rem(replica, 2)
    depth = replica // 2
    place = (1 - side) * depth + side * (ring - 1 - depth)
    step = 1 - 2 * lax.rem(me, 2)

    def member(position):
        position = lax.rem(position + 2 * ring, ring)
        late = position // (ring // 2)
        return (1 - late) * 2 * position + late * (2 * (ring - 1 - position) + 1)

    after = (member(place + step), me)
    before = (member(place - step), me)
    chunk = lambda hops: lax.rem(place - step * hops + 2 * ring, ring)
    greet(group_peers(replica, me, size) + [after, before])

    def reduce_copy(i, k):
        source = ins[i].at[chunk(1)] if k == 0 else lands[i].at[k - 1]
        return push(source, lands[i].at[k], r_send.at[i, k], r_recv.at[i, k], after)

    for i in range(n):
        reduce_copy(i, 0).start()
    for k in range(ring - 1):
        for i in range(n):
            reduce_copy(i, k).wait_recv()
            mine = ins[i][chunk(k + 2)].astype(jnp.float32)
            total = (mine + lands[i][k].astype(jnp.float32)).astype(lands[i].dtype)
            lands[i][k] = total
            if k < ring - 2:
                reduce_copy(i, k + 1).start()
            elif modes[i] == KEEP:
                outs[i][place] = total

    def swap_copy(i, k, source):
        target = lax.rem(me + k, size)
        return push(
            lands[i].at[ring - 2, target], swaps[i].at[source],
            s_send.at[i, k], s_recv.at[i, source], (replica, target),
        )

    for i in range(n):
        if modes[i] != KEEP:
            for k in range(1, size):
                swap_copy(i, k, me).start()
            swaps[i][me] = lands[i][ring - 2, me]

    def gather_copy(i, k):
        return push(
            outs[i].at[chunk(k)], outs[i].at[chunk(k)], a_send.at[i, k], a_recv.at[i, k], after
        )

    def arrival(i, k):
        return push(
            outs[i].at[chunk(k + 1)], outs[i].at[chunk(k + 1)], a_send.at[i, k], a_recv.at[i, k], after
        )

    order = [i for i in range(n) if modes[i] == KEEP] + [i for i in range(n) if modes[i] != KEEP]
    for i in order:
        if modes[i] != KEEP:
            for k in range(1, size):
                swap_copy(i, size - k, lax.rem(me + k, size)).wait_recv()
            if modes[i] == SWAP:
                outs[i][place] = swaps[i][...]
            else:
                outs[i][place] = jnp.sum(swaps[i][...], axis=0)
        gather_copy(i, 0).start()
    for k in range(ring - 1):
        for i in order:
            arrival(i, k).wait_recv()
            if k < ring - 2:
                gather_copy(i, k + 1).start()
    for i in range(n):
        for k in range(ring - 1):
            reduce_copy(i, k).wait_send()
            gather_copy(i, k).wait_send()
        if modes[i] != KEEP:
            for k in range(1, size):
                swap_copy(i, k, me).wait_send()


def closing(size, ring, arrays, modes):
    dma = pltpu.SemaphoreType.DMA
    n = len(arrays)
    shapes, lands, swaps = [], [], []
    for array, mode in zip(arrays, modes):
        out = array.shape if mode != ADD else array.shape[:1] + array.shape[2:]
        shapes.append(jax.ShapeDtypeStruct(out, array.dtype))
        lands.append(pltpu.VMEM((ring - 1,) + array.shape[1:], array.dtype))
        swaps.append(
            pltpu.VMEM(array.shape[1:] if mode != KEEP else (8, 128), array.dtype)
        )
    return pl.pallas_call(
        functools.partial(closing_kernel, size, ring, modes),
        out_shape=tuple(shapes),
        in_specs=vmem_specs(n),
        out_specs=tuple(vmem_specs(n)),
        scratch_shapes=lands + swaps + [
            dma((n, ring)), dma((n, ring)), dma((n, ring)), dma((n, ring)), dma((n, size)), dma((n, size)),
        ],
        compiler_params=pltpu.CompilerParams(
            collective_id=5, has_side_effects=True, vmem_limit_bytes=VMEM_LIMIT
        ),
    )(*arrays)


def local(
    ring,
    size,
    hidden_in,
    out_grad,
    lengths,
    norm1_gain,
    norm1_bias,
    qkv_weight,
    query_bias,
    value_bias,
    out_weight,
    out_bias,
    norm2_gain,
    norm2_bias,
    up_weight,
    up_bias,
    down_weight,
    down_bias,
):
    me = lax.axis_index("shard")
    rows, width = hidden_in.shape
    band = width // size
    seqs = lengths.shape[1]
    lane_count = max(band, 128)
    wide = lambda vector: jnp.pad(vector, (0, lane_count - vector.shape[0]))
    params = jnp.stack(
        [
            wide(v)
            for v in (
                norm1_gain, norm1_bias, out_bias, norm2_gain, norm2_bias, down_bias,
                lengths[0].astype(jnp.bfloat16), norm1_gain,
            )
        ]
    )
    qkv_parts = qkv_weight.reshape(2, band // 2, 3, size, band).transpose(3, 0, 1, 2, 4)
    qkv_parts = qkv_parts.reshape(size, 2, band // 2, 3 * band)
    ff_band = up_weight.shape[1] // size
    up_parts = up_weight.reshape(2, band // 2, size, ff_band).transpose(2, 0, 1, 3)
    hidden_all, upstream_all, params_all, qkv_all, up_all = opening(
        size, hidden_in, out_grad, params, qkv_parts, up_parts
    )
    hidden_all = hidden_all.reshape(size * rows, width)
    grad_all = upstream_all.reshape(size * rows, width)
    qkv_cols = qkv_all.reshape(width, 3 * band)
    up_cols = up_all.reshape(width, ff_band)
    gain_one, bias_one, outb_full, gain_two, bias_two, downb_full = (
        params_all[:, i, :band].reshape(width) for i in range(6)
    )
    lengths_all = params_all[:, 6, :seqs].astype(jnp.int32)
    mine = lambda array: lax.dynamic_slice_in_dim(array, me * band, band, axis=array.ndim - 1)
    own_rows = lambda array: lax.dynamic_slice_in_dim(array, me * rows, rows, axis=0)

    allowed = seq_mask(lengths_all, rows)
    inputs_wide = hidden_all.astype(jnp.float32)
    first_out, normed_one, inv_one = layer_norm(inputs_wide, gain_one, bias_one)
    first_in = first_out.astype(jnp.bfloat16)
    projected = product(first_in, qkv_cols)
    queries = (projected[:, :band] + query_bias.astype(jnp.float32)).astype(jnp.bfloat16)
    key_rows = projected[:, band : 2 * band].astype(jnp.bfloat16)
    values = (projected[:, 2 * band :] + value_bias.astype(jnp.float32)).astype(jnp.bfloat16)
    context, log_total = attend_forward(queries, key_rows, values, allowed)
    (attended,) = group_sum(
        size, [product(context, out_weight).astype(jnp.bfloat16)], (True,), 1
    )
    residual = (
        inputs_wide
        + attended.reshape(size * rows, width).astype(jnp.float32)
        + outb_full.astype(jnp.float32)
    )
    second_out, normed_two, inv_two = layer_norm(residual, gain_two, bias_two)
    second_in = second_out.astype(jnp.bfloat16)
    pre_act = product(second_in, up_cols) + up_bias.astype(jnp.float32)
    activ_value, gelu_slope = gelu_parts(pre_act)
    activated = activ_value.astype(jnp.bfloat16)
    down_part = product(activated, down_weight).astype(jnp.bfloat16)
    upstream = grad_all.astype(jnp.float32)
    pre_grad = right_product(grad_all, down_weight) * gelu_slope
    pre_round = pre_grad.astype(jnp.bfloat16)
    second_part = right_product(pre_round, up_cols).astype(jnp.bfloat16)
    second_sum, down_sum = group_sum(size, [second_part, down_part], (True, False), 2)
    hidden_out = (own_rows(residual) + down_sum + downb_full.astype(jnp.float32)).astype(
        jnp.bfloat16
    )
    down_grad = column_term(activated, grad_all).astype(jnp.bfloat16)
    up_grad = column_term(second_in, pre_round).astype(jnp.bfloat16)
    second_grad = second_sum.reshape(size * rows, width).astype(jnp.float32)
    norm_two_in, gain2_grad, bias2_grad = norm_back(second_grad, normed_two, inv_two, gain_two)
    resid_grad = upstream + norm_two_in
    resid_round = resid_grad.astype(jnp.bfloat16)
    outw_grad = column_term(context, resid_round).astype(jnp.bfloat16)
    context_grad = right_product(resid_round, out_weight).astype(jnp.bfloat16)
    query_grad, key_grad, value_grad = attend_backward(
        queries, key_rows, values, allowed, log_total, context_grad
    )
    qkv_grad = jnp.concatenate([query_grad, key_grad, value_grad], axis=1).astype(jnp.bfloat16)
    first_part = right_product(qkv_grad, qkv_cols).astype(jnp.bfloat16)
    (first_grad,) = group_sum(size, [first_part], (False,), 3)
    qkvw_grad = column_term(first_in, qkv_grad).astype(jnp.bfloat16)
    norm_one_in, gain1_grad, bias1_grad = norm_back(
        first_grad, own_rows(normed_one), own_rows(inv_one), gain_one
    )
    in_grad = (own_rows(resid_grad) + norm_one_in).astype(jnp.bfloat16)

    owned = jnp.concatenate(
        [
            jnp.sum(query_grad, axis=0),
            jnp.sum(value_grad, axis=0),
            mine(jnp.sum(resid_grad, axis=0)),
            mine(gain2_grad),
            mine(bias2_grad),
            jnp.sum(pre_grad, axis=0),
            mine(jnp.sum(upstream, axis=0)),
        ]
    )
    here = (jnp.arange(size) == me)[:, None]
    small = jnp.concatenate(
        [
            gain1_grad.reshape(size, band),
            bias1_grad.reshape(size, band),
            jnp.where(here, owned[None], 0.0),
        ],
        axis=1,
    )
    count = small.shape[1]
    small = small.reshape(size, ring, 1, count // ring).transpose(1, 0, 2, 3)
    slab = band // ring
    by_owner = lambda array: array.reshape(size, ring, slab, array.shape[1]).transpose(1, 0, 2, 3)
    down_all, outw_all, up_total, qkv_total, small_all = closing(
        size,
        ring,
        [
            down_grad.reshape(ring, -1, width),
            outw_grad.reshape(ring, -1, width),
            by_owner(up_grad),
            by_owner(qkvw_grad),
            small,
        ],
        (KEEP, KEEP, SWAP, SWAP, ADD),
    )
    downw_total = down_all.reshape(down_weight.shape).astype(jnp.float32)
    outw_total = outw_all.reshape(out_weight.shape).astype(jnp.float32)
    upw_total = up_total.transpose(0, 2, 1, 3).reshape(up_weight.shape).astype(jnp.float32)
    qkvw_total = (
        qkv_total.reshape(ring, size, slab, 3, band)
        .transpose(0, 2, 3, 1, 4)
        .reshape(qkv_weight.shape)
        .astype(jnp.float32)
    )
    flat = small_all.reshape(count)
    pieces = []
    offset = 0
    for length in (band, band, band, band, band, band, band, ff_band, band):
        pieces.append(flat[offset : offset + length])
        offset += length
    gain1_t, bias1_t, qbias_t, vbias_t, outb_t, gain2_t, bias2_t, upb_t, downb_t = pieces
    return (
        hidden_out,
        in_grad,
        gain1_t,
        bias1_t,
        qkvw_total,
        qbias_t,
        vbias_t,
        outw_total,
        outb_t,
        gain2_t,
        bias2_t,
        upw_total,
        upb_t,
        downw_total,
        downb_t,
    )


def solution(mesh):
    in_specs = (
        P(("replica", "shard"), None),
        P(("replica", "shard"), None),
        P(("replica", "shard"), None),
        P("shard"),
        P("shard"),
        P("shard", None),
        P("shard"),
        P("shard"),
        P("shard", None),
        P("shard"),
        P("shard"),
        P("shard"),
        P("shard", None),
        P("shard"),
        P("shard", None),
        P("shard"),
    )
    out_specs = (
        P(("replica", "shard"), None),
        P(("replica", "shard"), None),
        P("shard"),
        P("shard"),
        P("shard", None),
        P("shard"),
        P("shard"),
        P("shard", None),
        P("shard"),
        P("shard"),
        P("shard"),
        P("shard", None),
        P("shard"),
        P("shard", None),
        P("shard"),
    )
    body = functools.partial(local, mesh.shape["replica"], mesh.shape["shard"])
    return jax.shard_map(body, mesh=mesh, in_specs=in_specs, out_specs=out_specs, check_vma=False)
```
